32 devices in a mesh: row: 8 (over y, x, core), ctx: 4 (over z).
Axes of the slice: x: 2, y: 2, z: 4, core: 2. Of those that a mesh axis runs over, the one named last changes fastest.
Arguments:
- queries: bfloat16 [5, 4096, 128], P(None, ('row', 'ctx')), may hold values from -100 to 100
- keys: bfloat16 [4096, 128], P('ctx'), may hold values from -6 to 6
- doc_ids: int32 [64], replicated, may hold values from 0 to 3, never falling along the last dimension, each value on 1 to 48 neighbouring positions
- gate_query: bfloat16 [5, 128, 128], replicated, may hold values from -0.5 to 0.5
- gate_key: bfloat16 [384, 128], replicated, may hold values from -0.3125 to 0.3125
Outputs:
- block_map: float32 [5, 64, 64], P(None, ('row', 'ctx'))
- grad_query: float32 [5, 128, 128], replicated
- grad_key: float32 [384, 128], replicated
The draws below stay inside these ranges and needn't reach their ends.
Inputs may be any that keep to these rules, and one draw needn't show every extreme that they name: `doc_ids`: block document ids never fall along the sequence; each document spans 1 to 48 blocks and one spans exactly 48.
All inputs are finite; a program needn't handle non-finite values.
Results may differ from the reference program's by a relative error of at most 0.0003.
Values may be sent and summed in bfloat16 or wider, within the bound.
A program may use at most 64 MiB of HBM per device.

```python
import math
import jax
import jax.numpy as jnp
import numpy as np
from jax import lax

H = 5
HD = 128
DG = 128
BLK = 64
DOCS = 4
TOKENS = 4096
KB = 64
MOST = 48


def make_pair(key):
    base_key = jax.random.fold_in(key, 7)
    key_one, key_two = jax.random.split(base_key, 2)
    key_rows = jnp.clip(jax.random.normal(key_one, (TOKENS, HD), jnp.float32), -6.0, 6.0)
    query_rows = jnp.clip(jax.random.normal(key_two, (H, TOKENS, HD), jnp.float32), -6.0, 6.0)
    return (query_rows, key_rows)


def draw_queries(key, part):
    return make_pair(key)[0].astype(jnp.bfloat16)


def draw_keys(key, part):
    return make_pair(key)[1].astype(jnp.bfloat16)


def split_up(number_of, total, most, lean):
    portions = [(1 << 20) // math.isqrt(grade ** lean) + 1 for grade in range(2, number_of + 1)]
    spare, given = total - most - (number_of - 1), [1] * (number_of - 1)
    while spare > 0:
        free = [i for i in range(number_of - 1) if given[i] < most]
        pool, budget = sum([portions[i] for i in free]), spare
        for i in free:
            more = min(most - given[i], max(1, budget * portions[i] // pool), spare)
            given[i] = given[i] + more
            spare = spare - more
    return np.array([most] + given)


def ragged_sizes(key, amount, total, most, skew):
    if amount == 2:
        one = jax.random.randint(key, (), max(1, total - most), min(most, total - 1) + 1)
        return jnp.stack([one, total - one])
    sizes = jnp.asarray(split_up(amount, total, most, skew), jnp.int32)
    couples = (amount - 1) // 2
    giver, taker = sizes[1:1 + 2 * couples:2], sizes[2:2 + 2 * couples:2]
    room = jnp.minimum(giver - 1, most - taker)
    shifted = jax.random.randint(jax.random.fold_in(key, 1), (couples,), 0, 1 << 20) % (room + 1)
    sizes = sizes.at[1:1 + 2 * couples:2].set(giver - shifted).at[2:2 + 2 * couples:2].set(taker + shifted)
    return sizes[jax.random.permutation(jax.random.fold_in(key, 2), amount)]


def noise(key, dims, scale, reach, kind=jnp.bfloat16):
    return jnp.clip(scale * jax.random.normal(key, dims, jnp.float32), -reach, reach).astype(kind)


def setup_inputs(seed: int = 0) -> dict:
    splits = jax.random.split(jax.random.key(seed), 6)
    queries = draw_queries(jax.random.fold_in(splits[5], 71), 0)
    keys = draw_keys(jax.random.fold_in(splits[5], 71), 0)
    doc_ids = jnp.searchsorted(jnp.cumsum(ragged_sizes(splits[2], DOCS, KB, MOST, 2)), jnp.arange(KB), side="right").astype(jnp.int32)
    gate_query = noise(splits[3], (H, HD, DG), HD ** -0.5, 0.5)
    gate_key = noise(splits[4], (3 * HD, DG), (3 * HD) ** -0.5, 0.3125)
    return {"queries": queries, "keys": keys, "doc_ids": doc_ids, "gate_query": gate_query, "gate_key": gate_key}


NEG_FILL = -1e+30

def reference(queries, keys, doc_ids, gate_query, gate_key):
    score_scale = 1.0 / math.sqrt(HD)
    key_doc = jnp.repeat(doc_ids, BLK)
    key_pos = jnp.arange(TOKENS, dtype=jnp.int32)
    keys_wide = keys.astype(jnp.float32)

    def one_block(block_index):
        query_rows = lax.dynamic_slice_in_dim(queries, (block_index * BLK).astype(jnp.int32), BLK, 1).astype(jnp.float32)
        scores = jnp.einsum('hrd,kd->hrk', query_rows, keys_wide, precision=lax.Precision.HIGHEST) * score_scale
        query_pos = block_index * BLK + jnp.arange(BLK, dtype=jnp.int32)
        query_doc = doc_ids[block_index]
        allowed = (key_pos[None, :] <= query_pos[:, None]) & (key_doc[None, :] == query_doc)
        masked = jnp.where(allowed[None], scores, NEG_FILL)
        row_top = lax.optimization_barrier(jnp.max(masked, axis=2))
        row_total = lax.optimization_barrier(jnp.sum(jnp.where(allowed[None], jnp.exp(masked - row_top[:, :, None]), 0.0), axis=2))
        log_total = row_top + jnp.log(row_total)
        block_peaks = lax.optimization_barrier(jnp.max(masked.reshape(H, BLK, KB, BLK), axis=3))
        return lax.optimization_barrier(jnp.max(jnp.exp(block_peaks - log_total[:, :, None]), axis=1))
    block_map = jnp.transpose(lax.map(one_block, jnp.arange(KB, dtype=jnp.int32)), (1, 0, 2))
    query_pool = lax.optimization_barrier(jnp.mean(queries.astype(jnp.float32).reshape(H, KB, BLK, HD), axis=2))
    grouped = keys_wide.reshape(KB, BLK, HD)
    key_pool = jnp.concatenate([lax.optimization_barrier(jnp.max(grouped, axis=1)), lax.optimization_barrier(jnp.min(grouped, axis=1)), lax.optimization_barrier(jnp.mean(grouped, axis=1))], axis=1)
    query_gate = jnp.einsum('hbd,hde->hbe', query_pool, gate_query.astype(jnp.float32), precision=lax.Precision.HIGHEST)
    key_gate = jnp.dot(key_pool, gate_key.astype(jnp.float32), precision=lax.Precision.HIGHEST)
    gate_logits = jnp.einsum('hbe,ke->hbk', query_gate, key_gate, precision=lax.Precision.HIGHEST)
    blocks = jnp.arange(KB, dtype=jnp.int32)
    block_allowed = (blocks[None, :] <= blocks[:, None]) & (doc_ids[None, :] == doc_ids[:, None])
    gate_exp = jnp.where(block_allowed[None], jnp.exp(gate_logits), 0.0)
    gate_prob = gate_exp / lax.optimization_barrier(jnp.sum(gate_exp, axis=2, keepdims=True))
    target = block_map / lax.optimization_barrier(jnp.sum(block_map, axis=2, keepdims=True))
    diff = gate_prob - target
    query_back = jnp.einsum('hbk,ke->hbe', diff, key_gate, precision=lax.Precision.HIGHEST)
    grad_query = jnp.einsum('hbd,hbe->hde', query_pool, query_back, precision=lax.Precision.HIGHEST)
    key_back = jnp.einsum('hbk,hbe->ke', diff, query_gate, precision=lax.Precision.HIGHEST)
    grad_key = jnp.dot(key_pool.T, key_back, precision=lax.Precision.HIGHEST)
    return (block_map, grad_query, grad_key)
```

```python
import functools
import math

import jax
import jax.numpy as jnp
from jax import lax
from jax.experimental import pallas as pl
from jax.experimental.pallas import tpu as pltpu
from jax.sharding import PartitionSpec as P

BLK = 64
NEG = -1e30
PIECE = 16
LANES = 128
MESH = pl.DeviceIdType.MESH
HI = lax.Precision.HIGHEST


def fdot(a, b, dims):
    return lax.dot_general(a, b, (dims, ((), ())), precision=HI, preferred_element_type=jnp.float32)


def kernel(
    R, C, q_ref, k_ref, doc_ref, gq_ref, gk_ref,
    bm_ref, dq_ref, dk_ref,
    kbuf, q_t, peak, bsum, kpool, qp_own, diff_own, qp_all, diff_all,
    s1, s2, s3, rsem, small_send, small_recv,
):
    H, rows, D = q_ref.shape
    shard = k_ref.shape[0]
    nb = rows // BLK
    n = R * C
    TB = n * nb
    r = lax.axis_index("row")
    c = lax.axis_index("ctx")
    me = r * C + c
    core = lax.rem(r, 2)
    half = R // 2
    scale = 1.0 / math.sqrt(D)

    def ctx_peer(d):
        return lax.rem(c + d, C)

    def row_peer(d):
        return lax.rem(r + 2 * d, R)

    partner = r + 1 - 2 * core

    barrier = pltpu.get_barrier_semaphore()
    for d in range(1, C):
        pl.semaphore_signal(barrier, inc=1, device_id=(r, ctx_peer(d)), device_id_type=MESH)
    for d in range(1, half):
        pl.semaphore_signal(barrier, inc=1, device_id=(row_peer(d), c), device_id_type=MESH)
    pl.semaphore_signal(barrier, inc=1, device_id=(partner, c), device_id_type=MESH)

    qp_own[...] = jnp.zeros_like(qp_own)
    for h in range(H):
        qf = q_ref[h].astype(jnp.float32)
        q_t[:, h * rows:(h + 1) * rows] = qf.T.astype(jnp.bfloat16)
        for j in range(nb):
            qp_own[0, h * nb + j:h * nb + j + 1, :] = jnp.mean(
                qf[j * BLK:(j + 1) * BLK], axis=0, keepdims=True
            )
    peak[...] = jnp.full_like(peak, NEG)
    bsum[...] = jnp.zeros_like(bsum)
    if kpool.shape[1] > TB:
        kpool[...] = jnp.zeros_like(kpool)

    pl.semaphore_wait(barrier, C - 1 + half)

    def slot(cc, rr):
        return pl.ds(pl.multiple_of(cc * shard + rr * rows, rows), rows)

    def copy1(d):
        return pltpu.make_async_remote_copy(
            src_ref=k_ref.at[pl.ds(pl.multiple_of(r * rows, rows), rows)],
            dst_ref=kbuf.at[slot(c, r)],
            send_sem=s1.at[d], recv_sem=rsem.at[c * R + r],
            device_id=(r, ctx_peer(d)), device_id_type=MESH,
        )

    def copy2(d, e):
        cc = ctx_peer(d)
        return pltpu.make_async_remote_copy(
            src_ref=kbuf.at[slot(cc, r)], dst_ref=kbuf.at[slot(cc, r)],
            send_sem=s2.at[d * half + e], recv_sem=rsem.at[cc * R + r],
            device_id=(row_peer(e), c), device_id_type=MESH,
        )

    def copy3(d, e):
        cc, rr = ctx_peer(d), row_peer(e)
        return pltpu.make_async_remote_copy(
            src_ref=kbuf.at[slot(cc, rr)], dst_ref=kbuf.at[slot(cc, rr)],
            send_sem=s3.at[d * half + e], recv_sem=rsem.at[cc * R + rr],
            device_id=(partner, c), device_id_type=MESH,
        )

    def arrived(cc, rr):
        pltpu.make_async_copy(
            kbuf.at[slot(cc, rr)], kbuf.at[slot(cc, rr)], rsem.at[cc * R + rr]
        ).wait()

    for d in range(1, C):
        copy1(d).start()

    a0 = me * nb
    lane = lax.broadcasted_iota(jnp.int32, (1, rows), 1)
    qdoc = jnp.zeros((1, rows), jnp.int32)
    for j in range(nb):
        qdoc = jnp.where(lane // BLK == j, doc_ref[a0 + j], qdoc)

    def score(num, keys, diagonal):
        for h in range(H):
            s = jnp.dot(
                keys, q_t[:, h * rows:(h + 1) * rows], preferred_element_type=jnp.float32
            ) * scale
            if diagonal:
                ki = lax.broadcasted_iota(jnp.int32, (rows, rows), 0)
                qi = lax.broadcasted_iota(jnp.int32, (rows, rows), 1)
                s = jnp.where(ki <= qi, s, NEG)
            for j in range(nb):
                b = num * nb + j
                t = s[j * BLK:(j + 1) * BLK]
                top = jnp.max(t, axis=0, keepdims=True)
                total = jnp.sum(jnp.exp(t - top), axis=0, keepdims=True)
                peak[h, pl.ds(b, 1), :] = jnp.where(
                    qdoc == doc_ref[b], top, NEG
                )
                bsum[h, pl.ds(b, 1), :] = total

    def process(cc, rr):
        num = cc * R + rr
        keys = kbuf[slot(cc, rr), :]
        wide = keys.astype(jnp.float32)
        for j in range(nb):
            t = wide[j * BLK:(j + 1) * BLK]
            b = num * nb + j
            kpool[0, pl.ds(b, 1), :] = jnp.max(t, axis=0, keepdims=True)
            kpool[1, pl.ds(b, 1), :] = jnp.min(t, axis=0, keepdims=True)
            kpool[2, pl.ds(b, 1), :] = jnp.mean(t, axis=0, keepdims=True)

        @pl.when(num < me)
        def _():
            score(num, keys, False)

        @pl.when(num == me)
        def _():
            score(num, keys, True)

    kbuf[pl.ds(pl.multiple_of(c * shard, shard), shard), :] = k_ref[...]

    @pl.loop(0, R)
    def _(i):
        process(c, i)

    @pl.loop(1, C)
    def _(d):
        arrived(ctx_peer(d), r)
        for e in range(1, half):
            copy2(d, e).start()
        copy3(d, 0).start()

    @pl.loop(1, C)
    def _(d):
        process(ctx_peer(d), r)

    @pl.loop(1, C)
    def _(d):
        @pl.loop(1, half)
        def _(e):
            arrived(ctx_peer(d), row_peer(e))
            copy3(d, e).start()

    @pl.loop(0, (C - 1) * (half - 1))
    def _(i):
        process(ctx_peer(i // (half - 1) + 1), row_peer(i % (half - 1) + 1))

    other = partner

    @pl.loop(0, (C - 1) * half)
    def _(i):
        arrived(ctx_peer(i // half + 1), lax.rem(other + 2 * (i % half), R))

    def small(k, own, everyone, p):
        to = lax.rem(me + p, n)
        return pltpu.make_async_remote_copy(
            src_ref=own,
            dst_ref=everyone.at[:, pl.ds(pl.multiple_of(me * PIECE, PIECE), PIECE)],
            send_sem=small_send.at[k], recv_sem=small_recv.at[k],
            device_id=(to // C, to % C), device_id_type=MESH,
        )

    def small_wait(k, everyone):
        part = everyone.at[:, pl.ds(0, (n - 1) * PIECE)]
        pltpu.make_async_copy(part, part, small_recv.at[k]).wait()

    def small_sent(k, everyone):
        part = everyone.at[:, pl.ds(0, (n - 1) * PIECE)]
        pltpu.make_async_copy(part, part, small_send.at[k]).wait()

    @pl.loop(1, n)
    def _(p):
        small(0, qp_own, qp_all, p).start()

    @pl.loop(0, (C - 1) * half)
    def _(i):
        process(ctx_peer(i // half + 1), lax.rem(other + 2 * (i % half), R))

    own_rows = pl.ds(pl.multiple_of(me * PIECE, PIECE), PIECE)
    qp_all[0, own_rows, :] = qp_own[0]

    gk = gk_ref[...].astype(jnp.float32)
    pooled = jnp.concatenate([kpool[0], kpool[1], kpool[2]], axis=1)
    key_gate = fdot(pooled, gk, ((1,), (0,)))
    row16 = lax.broadcasted_iota(jnp.int32, (PIECE, 1), 0)
    qg = jnp.zeros((PIECE, D), jnp.float32)
    for h in range(H):
        t = fdot(qp_own[0], gq_ref[h].astype(jnp.float32), ((1,), (0,)))
        qg = jnp.where(row16 // nb == h, t, qg)
    logits = fdot(qg, key_gate, ((1,), (1,)))

    width = peak.shape[1]
    maps = jnp.full((PIECE, width), NEG, jnp.float32)
    for h in range(H):
        pk = peak[h]
        top = jnp.max(pk, axis=0, keepdims=True)
        total = jnp.sum(bsum[h] * jnp.exp(pk - top), axis=0, keepdims=True)
        chance = (pk - (top + jnp.log(total))).T
        for j in range(nb):
            best = jnp.max(chance[j * BLK:(j + 1) * BLK], axis=0, keepdims=True)
            maps = jnp.where(row16 == h * nb + j, best, maps)
    allowed = maps > 0.1 * NEG
    block_map = jnp.where(allowed, jnp.exp(maps), 0.0)
    for h in range(H):
        for j in range(nb):
            bm_ref[h, j:j + 1, :] = block_map[h * nb + j:h * nb + j + 1, :TB]
    used = row16 < H * nb
    gate_exp = jnp.where(allowed, jnp.exp(logits), 0.0)
    gate_sum = jnp.where(used, jnp.sum(gate_exp, axis=1, keepdims=True), 1.0)
    map_sum = jnp.where(used, jnp.sum(block_map, axis=1, keepdims=True), 1.0)
    diff = gate_exp / gate_sum - block_map / map_sum
    for w in range(width // LANES):
        diff_own[w] = diff[:, w * LANES:(w + 1) * LANES]

    @pl.loop(1, n)
    def _(p):
        small(1, diff_own, diff_all, p).start()

    diff_all[:, own_rows, :] = diff_own[...]

    small_wait(0, qp_all)
    qgs = []
    qps = []
    for h in range(H):
        qp = jnp.concatenate(
            [qp_all[0, pl.ds(h * nb + j, n, stride=PIECE), :] for j in range(nb)], axis=0
        )
        qps.append(qp)
        qgs.append(fdot(qp, gq_ref[h].astype(jnp.float32), ((1,), (0,))))

    small_wait(1, diff_all)
    key_back = jnp.zeros((width, D), jnp.float32)
    for h in range(H):
        parts = []
        for j in range(nb):
            at = pl.ds(h * nb + j, n, stride=PIECE)
            parts.append(jnp.concatenate(
                [diff_all[w, at, :] for w in range(width // LANES)], axis=1
            ))
        diff = jnp.concatenate(parts, axis=0)
        back = fdot(diff, key_gate, ((1,), (0,)))
        dq_ref[h] = fdot(qps[h], back, ((0,), (0,)))
        key_back = key_back + fdot(diff, qgs[h], ((0,), (0,)))
    dk_ref[...] = fdot(pooled, key_back, ((0,), (0,)))

    small_sent(0, qp_all)
    small_sent(1, diff_all)
    for d in range(1, C):
        copy1(d).wait_send()

        @pl.loop(0, half)
        def _(e):
            copy3(d, e).wait_send()

            @pl.when(e > 0)
            def _():
                copy2(d, e).wait_send()


def shards(R, C, queries, keys, doc_ids, gate_query, gate_key):
    H, rows, D = queries.shape
    n = R * C
    nb = rows // BLK
    TB = doc_ids.shape[0]
    width = -(-TB // LANES) * LANES
    half = R // 2
    vm = pl.BlockSpec(memory_space=pltpu.VMEM)
    sm = pl.BlockSpec(memory_space=pltpu.SMEM)
    dma = pltpu.SemaphoreType.DMA
    return pl.pallas_call(
        functools.partial(kernel, R, C),
        out_shape=(
            jax.ShapeDtypeStruct((H, nb, TB), jnp.float32),
            jax.ShapeDtypeStruct((H, D, gate_query.shape[2]), jnp.float32),
            jax.ShapeDtypeStruct(gate_key.shape, jnp.float32),
        ),
        in_specs=[vm, vm, sm, vm, vm],
        out_specs=(vm, vm, vm),
        scratch_shapes=[
            pltpu.VMEM((C * keys.shape[0], D), jnp.bfloat16),
            pltpu.VMEM((D, H * rows), jnp.bfloat16),
            pltpu.VMEM((H, width, rows), jnp.float32),
            pltpu.VMEM((H, width, rows), jnp.float32),
            pltpu.VMEM((3, width, D), jnp.float32),
            pltpu.VMEM((1, PIECE, D), jnp.float32),
            pltpu.VMEM((width // LANES, PIECE, LANES), jnp.float32),
            pltpu.VMEM((1, n * PIECE, D), jnp.float32),
            pltpu.VMEM((width // LANES, n * PIECE, LANES), jnp.float32),
            dma((C,)), dma((C * half,)), dma((C * half,)), dma((n,)),
            dma((2,)), dma((2,)),
        ],
        compiler_params=pltpu.CompilerParams(
            collective_id=0, has_side_effects=True, vmem_limit_bytes=60 * 1024 * 1024
        ),
    )(queries, keys, doc_ids, gate_query, gate_key)


def solution(mesh):
    R, C = mesh.shape["row"], mesh.shape["ctx"]
    in_specs = (P(None, ("row", "ctx"), None), P("ctx", None), P(), P(), P())
    out_specs = (P(None, ("row", "ctx"), None), P(), P())
    return jax.shard_map(
        functools.partial(shards, R, C), mesh=mesh, in_specs=in_specs, out_specs=out_specs,
        check_vma=False,
    )
```

```python
import functools
import math

import jax
import jax.numpy as jnp
from jax import lax
from jax.experimental import pallas as pl
from jax.experimental.pallas import tpu as pltpu
from jax.sharding import PartitionSpec as P

BLK = 64
NEG = -1e30
PIECE = 16
MESH = pl.DeviceIdType.MESH
HI = lax.Precision.HIGHEST


def fdot(a, b, dims):
    return lax.dot_general(a, b, (dims, ((), ())), precision=HI, preferred_element_type=jnp.float32)


def kernel(
    R, C, q_ref, k_ref, doc_ref, gq_ref, gk_ref,
    bm_ref, dq_ref, dk_ref,
    kbuf, q_t, peak, bsum, pieces, diff_own, diff_all,
    s1, s2, s3, rsem, ps1, ps2, ps3, pctx, prow, small_send, small_recv,
):
    H, rows, D = q_ref.shape
    shard = k_ref.shape[0]
    nb = rows // BLK
    n = R * C
    TB = n * nb
    r = lax.axis_index("row")
    c = lax.axis_index("ctx")
    me = r * C + c
    half = R // 2
    scale = 1.0 / math.sqrt(D)
    used = H * nb

    def ctx_peer(d):
        return lax.rem(c + d, C)

    def row_peer(d):
        return lax.rem(r + 2 * d, R)

    partner = r + 1 - 2 * lax.rem(r, 2)

    def other_row(e):
        return lax.rem(partner + 2 * e, R)

    def needs(rr, cc):
        return cc * R < (rr // 2 + 1) * 2 * C

    barrier = pltpu.get_barrier_semaphore()
    for d in range(1, C):
        pl.semaphore_signal(barrier, inc=1, device_id=(r, ctx_peer(d)), device_id_type=MESH)
    for d in range(1, half):
        pl.semaphore_signal(barrier, inc=1, device_id=(row_peer(d), c), device_id_type=MESH)
    pl.semaphore_signal(barrier, inc=1, device_id=(partner, c), device_id_type=MESH)

    def slot(cc, rr):
        return pl.ds(pl.multiple_of(cc * shard + rr * rows, rows), rows)

    def part(rr):
        return pl.ds(pl.multiple_of(rr * PIECE, PIECE), PIECE)

    for h in range(H):
        qf = q_ref[h].astype(jnp.float32)
        q_t[:, h * rows:(h + 1) * rows] = qf.T.astype(jnp.bfloat16)
        for j in range(nb):
            pieces[c, pl.ds(r * PIECE + h * nb + j, 1), :] = jnp.mean(
                qf[j * BLK:(j + 1) * BLK], axis=0, keepdims=True
            )
    wide = k_ref[pl.ds(pl.multiple_of(r * rows, rows), rows), :].astype(jnp.float32)
    for j in range(nb):
        t = wide[j * BLK:(j + 1) * BLK]
        for i, pool in enumerate((jnp.max, jnp.min, jnp.mean)):
            pieces[c, pl.ds(r * PIECE + used + i * nb + j, 1), :] = pool(
                t, axis=0, keepdims=True
            )
    peak[...] = jnp.full_like(peak, NEG)
    bsum[...] = jnp.zeros_like(bsum)

    pl.semaphore_wait(barrier, C - 1 + half)

    def copy1(d):
        return pltpu.make_async_remote_copy(
            src_ref=k_ref.at[pl.ds(pl.multiple_of(r * rows, rows), rows)],
            dst_ref=kbuf.at[slot(c, r)],
            send_sem=s1.at[d], recv_sem=rsem.at[c * R + r],
            device_id=(r, ctx_peer(d)), device_id_type=MESH,
        )

    def copy2(d, e):
        cc = ctx_peer(d)
        return pltpu.make_async_remote_copy(
            src_ref=kbuf.at[slot(cc, r)], dst_ref=kbuf.at[slot(cc, r)],
            send_sem=s2.at[d * half + e], recv_sem=rsem.at[cc * R + r],
            device_id=(row_peer(e), c), device_id_type=MESH,
        )

    def copy3(d, e):
        cc, rr = ctx_peer(d), row_peer(e)
        return pltpu.make_async_remote_copy(
            src_ref=kbuf.at[slot(cc, rr)], dst_ref=kbuf.at[slot(cc, rr)],
            send_sem=s3.at[d * half + e], recv_sem=rsem.at[cc * R + rr],
            device_id=(partner, c), device_id_type=MESH,
        )

    def arrived(cc, rr):
        pltpu.make_async_copy(
            kbuf.at[slot(cc, rr)], kbuf.at[slot(cc, rr)], rsem.at[cc * R + rr]
        ).wait()

    def piece1(d):
        return pltpu.make_async_remote_copy(
            src_ref=pieces.at[c, part(r)], dst_ref=pieces.at[c, part(r)],
            send_sem=ps1.at[d], recv_sem=pctx.at[c],
            device_id=(r, ctx_peer(d)), device_id_type=MESH,
        )

    def piece2(e):
        return pltpu.make_async_remote_copy(
            src_ref=pieces.at[:, part(r)], dst_ref=pieces.at[:, part(r)],
            send_sem=ps2.at[e], recv_sem=prow.at[r],
            device_id=(row_peer(e), c), device_id_type=MESH,
        )

    def piece3(e):
        rr = row_peer(e)
        return pltpu.make_async_remote_copy(
            src_ref=pieces.at[:, part(rr)], dst_ref=pieces.at[:, part(rr)],
            send_sem=ps3.at[e], recv_sem=prow.at[rr],
            device_id=(partner, c), device_id_type=MESH,
        )

    def row_arrived(rr):
        pltpu.make_async_copy(
            pieces.at[:, part(rr)], pieces.at[:, part(rr)], prow.at[rr]
        ).wait()

    for d in range(1, C):
        copy1(d).start()
    for d in range(1, C):
        piece1(d).start()

    a0 = me * nb
    lane = lax.broadcasted_iota(jnp.int32, (1, rows), 1)
    qdoc = jnp.zeros((1, rows), jnp.int32)
    for j in range(nb):
        qdoc = jnp.where(lane // BLK == j, doc_ref[a0 + j], qdoc)

    def score(num, keys, diagonal):
        for h in range(H):
            s = jnp.dot(
                keys, q_t[:, h * rows:(h + 1) * rows], preferred_element_type=jnp.float32
            ) * scale
            if diagonal:
                ki = lax.broadcasted_iota(jnp.int32, (rows, rows), 0)
                qi = lax.broadcasted_iota(jnp.int32, (rows, rows), 1)
                s = jnp.where(ki <= qi, s, NEG)
            for j in range(nb):
                b = num * nb + j
                t = s[j * BLK:(j + 1) * BLK]
                top = jnp.max(t, axis=0, keepdims=True)
                total = jnp.sum(jnp.exp(t - top), axis=0, keepdims=True)
                peak[h, pl.ds(b, 1), :] = jnp.where(qdoc == doc_ref[b], top, NEG)
                bsum[h, pl.ds(b, 1), :] = total

    def process(ref, at, num):
        @pl.when(num < me)
        def _():
            score(num, ref[at, :], False)

        @pl.when(num == me)
        def _():
            score(num, ref[at, :], True)

    @pl.loop(0, R)
    def _(i):
        process(k_ref, pl.ds(pl.multiple_of(i * rows, rows), rows), c * R + i)

    for d in range(1, C):
        cc = ctx_peer(d)
        arrived(cc, r)
        for e in range(1, half):
            @pl.when(needs(row_peer(e), cc))
            def _():
                copy2(d, e).start()

        @pl.when(needs(r, cc))
        def _():
            copy3(d, 0).start()

    for d in range(1, C):
        cc = ctx_peer(d)
        pltpu.make_async_copy(pieces.at[cc, part(r)], pieces.at[cc, part(r)], pctx.at[cc]).wait()
    for e in range(1, half):
        piece2(e).start()
    piece3(0).start()

    @pl.loop(1, C)
    def _(d):
        process(kbuf, slot(ctx_peer(d), r), ctx_peer(d) * R + r)

    @pl.loop(1, C)
    def _(d):
        @pl.when(needs(r, ctx_peer(d)))
        def _():
            @pl.loop(1, half)
            def _(e):
                arrived(ctx_peer(d), row_peer(e))
                copy3(d, e).start()

    for e in range(1, half):
        row_arrived(row_peer(e))
        piece3(e).start()

    @pl.loop(0, (C - 1) * (half - 1))
    def _(i):
        cc, rr = ctx_peer(i // (half - 1) + 1), row_peer(i % (half - 1) + 1)
        process(kbuf, slot(cc, rr), cc * R + rr)

    @pl.loop(0, (C - 1) * half)
    def _(i):
        cc, rr = ctx_peer(i // half + 1), other_row(i % half)

        @pl.when(needs(r, cc))
        def _():
            arrived(cc, rr)

        process(kbuf, slot(cc, rr), cc * R + rr)

    for e in range(half):
        row_arrived(other_row(e))

    def gathered(j):
        return jnp.concatenate(
            [pieces[i, pl.ds(j, R, stride=PIECE), :] for i in range(C)], axis=0
        )

    lanes_k = []
    for i in range(3):
        halves = [gathered(used + i * nb + j) for j in range(nb)]
        lanes_k.append(jnp.stack(halves, axis=1).reshape(TB, D))
    pooled = jnp.concatenate(lanes_k, axis=1)
    key_gate = fdot(pooled, gk_ref[...].astype(jnp.float32), ((1,), (0,)))
    row16 = lax.broadcasted_iota(jnp.int32, (PIECE, 1), 0)
    own = pieces[c, part(r), :]
    qg = jnp.zeros((PIECE, D), jnp.float32)
    qps, qgs = [], []
    for h in range(H):
        gate = gq_ref[h].astype(jnp.float32)
        qg = jnp.where(row16 // nb == h, fdot(own, gate, ((1,), (0,))), qg)
    logits = fdot(qg, key_gate, ((1,), (1,)))

    maps = jnp.full((PIECE, TB), NEG, jnp.float32)
    for h in range(H):
        pk = peak[h]
        top = jnp.max(pk, axis=0, keepdims=True)
        total = jnp.sum(bsum[h] * jnp.exp(pk - top), axis=0, keepdims=True)
        chance = (pk - (top + jnp.log(total))).T
        for j in range(nb):
            best = jnp.max(chance[j * BLK:(j + 1) * BLK], axis=0, keepdims=True)
            maps = jnp.where(row16 == h * nb + j, best, maps)
    allowed = maps > 0.1 * NEG
    block_map = jnp.where(allowed, jnp.exp(maps), 0.0)
    live = row16 < used
    gate_exp = jnp.where(allowed, jnp.exp(logits), 0.0)
    gate_sum = jnp.where(live, jnp.sum(gate_exp, axis=1, keepdims=True), 1.0)
    map_sum = jnp.where(live, jnp.sum(block_map, axis=1, keepdims=True), 1.0)
    diff = gate_exp / gate_sum - block_map / map_sum
    for h in range(H):
        for j in range(nb):
            diff_own[h:h + 1, j * TB:(j + 1) * TB] = diff[h * nb + j:h * nb + j + 1, :]

    place = c * R + r

    def send(p):
        to = lax.rem(place + p, n)
        return pltpu.make_async_remote_copy(
            src_ref=diff_own, dst_ref=diff_all.at[place],
            send_sem=small_send.at[0], recv_sem=small_recv.at[0],
            device_id=(to % R, to // R), device_id_type=MESH,
        )

    @pl.loop(1, n)
    def _(p):
        send(p).start()

    diff_all[place] = diff_own[...]
    for h in range(H):
        for j in range(nb):
            bm_ref[h, j:j + 1, :] = block_map[h * nb + j:h * nb + j + 1, :]

    for h in range(H):
        qp = jnp.concatenate([gathered(h * nb + j) for j in range(nb)], axis=0)
        qps.append(qp)
        qgs.append(fdot(qp, gq_ref[h].astype(jnp.float32), ((1,), (0,))))

    both = jnp.concatenate([key_gate] * nb, axis=0)
    wide_lane = lax.broadcasted_iota(jnp.int32, (1, nb * TB), 1)
    rest = diff_all.at[pl.ds(0, n - 1)]
    pltpu.make_async_copy(rest, rest, small_recv.at[0]).wait()
    key_back = jnp.zeros((nb * TB, D), jnp.float32)
    for h in range(H):
        mixed = diff_all[:, h, :]
        diff = jnp.concatenate(
            [jnp.where(wide_lane // TB == j, mixed, 0.0) for j in range(nb)], axis=0
        )
        back = fdot(diff, both, ((1,), (0,)))
        dq_ref[h] = fdot(qps[h], back, ((0,), (0,)))
        key_back = key_back + fdot(diff, qgs[h], ((0,), (0,)))
    folded = key_back[:TB]
    for j in range(1, nb):
        folded = folded + key_back[j * TB:(j + 1) * TB]
    dk_ref[...] = fdot(pooled, folded, ((0,), (0,)))

    pltpu.make_async_copy(rest, rest, small_send.at[0]).wait()
    for d in range(1, C):
        cc = ctx_peer(d)
        copy1(d).wait_send()
        piece1(d).wait_send()
        for e in range(half):
            @pl.when(needs(r, cc))
            def _():
                copy3(d, e).wait_send()

            if e > 0:
                @pl.when(needs(row_peer(e), cc))
                def _():
                    copy2(d, e).wait_send()
    for e in range(half):
        piece3(e).wait_send()
        if e > 0:
            piece2(e).wait_send()


def shards(R, C, queries, keys, doc_ids, gate_query, gate_key):
    H, rows, D = queries.shape
    n = R * C
    nb = rows // BLK
    TB = doc_ids.shape[0]
    half = R // 2
    vm = pl.BlockSpec(memory_space=pltpu.VMEM)
    sm = pl.BlockSpec(memory_space=pltpu.SMEM)
    dma = pltpu.SemaphoreType.DMA
    return pl.pallas_call(
        functools.partial(kernel, R, C),
        out_shape=(
            jax.ShapeDtypeStruct((H, nb, TB), jnp.float32),
            jax.ShapeDtypeStruct((H, D, gate_query.shape[2]), jnp.float32),
            jax.ShapeDtypeStruct(gate_key.shape, jnp.float32),
        ),
        in_specs=[vm, vm, sm, vm, vm],
        out_specs=(vm, vm, vm),
        scratch_shapes=[
            pltpu.VMEM((C * keys.shape[0], D), jnp.bfloat16),
            pltpu.VMEM((D, H * rows), jnp.bfloat16),
            pltpu.VMEM((H, TB, rows), jnp.float32),
            pltpu.VMEM((H, TB, rows), jnp.float32),
            pltpu.VMEM((C, R * PIECE, D), jnp.float32),
            pltpu.VMEM((H, nb * TB), jnp.float32),
            pltpu.VMEM((n, H, nb * TB), jnp.float32),
            dma((C,)), dma((C * half,)), dma((C * half,)), dma((n,)),
            dma((C,)), dma((half,)), dma((half,)), dma((C,)), dma((R,)),
            dma((1,)), dma((1,)),
        ],
        compiler_params=pltpu.CompilerParams(
            collective_id=0, has_side_effects=True, vmem_limit_bytes=60 * 1024 * 1024
        ),
    )(queries, keys, doc_ids, gate_query, gate_key)


def solution(mesh):
    R, C = mesh.shape["row"], mesh.shape["ctx"]
    in_specs = (P(None, ("row", "ctx"), None), P("ctx", None), P(), P(), P())
    out_specs = (P(None, ("row", "ctx"), None), P(), P())
    return jax.shard_map(
        functools.partial(shards, R, C), mesh=mesh, in_specs=in_specs, out_specs=out_specs,
        check_vma=False,
    )
```

```python
import functools
import math

import jax
import jax.numpy as jnp
from jax import lax
from jax.experimental import pallas as pl
from jax.experimental.pallas import tpu as pltpu
from jax.sharding import PartitionSpec as P

BLK = 64
NEG = -1e30
PIECE = 16
GROUP = 4
MESH = pl.DeviceIdType.MESH
HI = lax.Precision.HIGHEST


def fdot(a, b, dims):
    return lax.dot_general(a, b, (dims, ((), ())), precision=HI, preferred_element_type=jnp.float32)


def kernel(
    R, C, q_ref, k_ref, doc_ref, gq_ref, gk_ref,
    bm_ref, dq_ref, dk_ref,
    kbuf, q_t, peak, bsum, pieces, diff_own, diff_all,
    s1, s2, s3, rsem, ps1, ps2, ps3, pctx, prow, ds1, ds2, dctx, drow,
):
    H, rows, D = q_ref.shape
    shard = k_ref.shape[0]
    nb = rows // BLK
    n = R * C
    TB = n * nb
    r = lax.axis_index("row")
    c = lax.axis_index("ctx")
    me = r * C + c
    half = R // 2
    scale = 1.0 / math.sqrt(D)
    used = H * nb

    def ctx_peer(d):
        return lax.rem(c + d, C)

    def row_peer(d):
        return lax.rem(r + 2 * d, R)

    partner = r + 1 - 2 * lax.rem(r, 2)

    def other_row(e):
        return lax.rem(partner + 2 * e, R)

    def needs(rr, cc):
        return cc * R < (rr // 2 + 1) * 2 * C

    barrier = pltpu.get_barrier_semaphore()
    for d in range(1, C):
        pl.semaphore_signal(barrier, inc=1, device_id=(r, ctx_peer(d)), device_id_type=MESH)
    for d in range(1, half):
        pl.semaphore_signal(barrier, inc=1, device_id=(row_peer(d), c), device_id_type=MESH)
    pl.semaphore_signal(barrier, inc=1, device_id=(partner, c), device_id_type=MESH)

    def slot(cc, rr):
        return pl.ds(pl.multiple_of(cc * shard + rr * rows, rows), rows)

    def part(rr):
        return pl.ds(pl.multiple_of(rr * PIECE, PIECE), PIECE)

    for h in range(H):
        qf = q_ref[h].astype(jnp.float32)
        q_t[:, h * rows:(h + 1) * rows] = qf.T.astype(jnp.bfloat16)
        for j in range(nb):
            pieces[c, pl.ds(r * PIECE + h * nb + j, 1), :] = jnp.mean(
                qf[j * BLK:(j + 1) * BLK], axis=0, keepdims=True
            )
    wide = k_ref[pl.ds(pl.multiple_of(r * rows, rows), rows), :].astype(jnp.float32)
    for j in range(nb):
        t = wide[j * BLK:(j + 1) * BLK]
        for i, pool in enumerate((jnp.max, jnp.min, jnp.mean)):
            pieces[c, pl.ds(r * PIECE + used + i * nb + j, 1), :] = pool(
                t, axis=0, keepdims=True
            )
    peak[...] = jnp.full_like(peak, NEG)
    bsum[...] = jnp.zeros_like(bsum)

    a0 = me * nb
    lane = lax.broadcasted_iota(jnp.int32, (1, rows), 1)
    qdoc = jnp.zeros((1, rows), jnp.int32)
    for j in range(nb):
        qdoc = jnp.where(lane // BLK == j, doc_ref[a0 + j], qdoc)

    def score(num, keys, diagonal):
        for h in range(H):
            s = jnp.dot(
                keys, q_t[:, h * rows:(h + 1) * rows], preferred_element_type=jnp.float32
            )
            if diagonal:
                ki = lax.broadcasted_iota(jnp.int32, (rows, rows), 0)
                qi = lax.broadcasted_iota(jnp.int32, (rows, rows), 1)
                s = jnp.where(ki <= qi, s, NEG)
            for j in range(keys.shape[0] // BLK):
                b = num * nb + j
                t = s[j * BLK:(j + 1) * BLK]
                top = jnp.max(t, axis=0, keepdims=True)
                total = jnp.sum(
                    jnp.exp2((t - top) * (scale * math.log2(math.e))), axis=0, keepdims=True
                )
                peak[h, pl.ds(b, 1), :] = jnp.where(qdoc == doc_ref[b], top * scale, NEG)
                bsum[h, pl.ds(b, 1), :] = total

    group = math.gcd(R, GROUP)

    def process(ref, base, first):
        @pl.when(first + group <= me)
        def _():
            for i in range(0, group, 2):
                at = pl.multiple_of(base + i * rows, rows)
                score(first + i, ref[pl.ds(at, 2 * rows), :], False)

        @pl.when(first + group > me)
        def _():
            @pl.loop(0, group)
            def _(i):
                at = pl.ds(pl.multiple_of(base + i * rows, rows), rows)

                @pl.when(first + i < me)
                def _():
                    score(first + i, ref[at, :], False)

                @pl.when(first + i == me)
                def _():
                    score(first + i, ref[at, :], True)

    @pl.loop(0, R // group)
    def _(g):
        process(k_ref, g * group * rows, c * R + g * group)

    pl.semaphore_wait(barrier, C - 1 + half)

    def copy1(d):
        return pltpu.make_async_remote_copy(
            src_ref=k_ref.at[pl.ds(pl.multiple_of(r * rows, rows), rows)],
            dst_ref=kbuf.at[slot(c, r)],
            send_sem=s1.at[d], recv_sem=rsem.at[c * R + r],
            device_id=(r, ctx_peer(d)), device_id_type=MESH,
        )

    def copy2(d, e):
        cc = ctx_peer(d)
        return pltpu.make_async_remote_copy(
            src_ref=kbuf.at[slot(cc, r)], dst_ref=kbuf.at[slot(cc, r)],
            send_sem=s2.at[d * half + e], recv_sem=rsem.at[cc * R + r],
            device_id=(row_peer(e), c), device_id_type=MESH,
        )

    def copy3(d, e):
        cc, rr = ctx_peer(d), row_peer(e)
        return pltpu.make_async_remote_copy(
            src_ref=kbuf.at[slot(cc, rr)], dst_ref=kbuf.at[slot(cc, rr)],
            send_sem=s3.at[d * half + e], recv_sem=rsem.at[cc * R + rr],
            device_id=(partner, c), device_id_type=MESH,
        )

    def arrived(cc, rr):
        pltpu.make_async_copy(
            kbuf.at[slot(cc, rr)], kbuf.at[slot(cc, rr)], rsem.at[cc * R + rr]
        ).wait()

    def piece1(d):
        return pltpu.make_async_remote_copy(
            src_ref=pieces.at[c, part(r)], dst_ref=pieces.at[c, part(r)],
            send_sem=ps1.at[d], recv_sem=pctx.at[c],
            device_id=(r, ctx_peer(d)), device_id_type=MESH,
        )

    def piece2(e):
        return pltpu.make_async_remote_copy(
            src_ref=pieces.at[:, part(r)], dst_ref=pieces.at[:, part(r)],
            send_sem=ps2.at[e], recv_sem=prow.at[r],
            device_id=(row_peer(e), c), device_id_type=MESH,
        )

    def piece3(e):
        rr = row_peer(e)
        return pltpu.make_async_remote_copy(
            src_ref=pieces.at[:, part(rr)], dst_ref=pieces.at[:, part(rr)],
            send_sem=ps3.at[e], recv_sem=prow.at[rr],
            device_id=(partner, c), device_id_type=MESH,
        )

    def row_arrived(rr):
        pltpu.make_async_copy(
            pieces.at[:, part(rr)], pieces.at[:, part(rr)], prow.at[rr]
        ).wait()

    for d in range(1, C):
        copy1(d).start()
    for d in range(1, C):
        piece1(d).start()

    for d in range(1, C):
        cc = ctx_peer(d)
        arrived(cc, r)
        for e in range(1, half):
            @pl.when(needs(row_peer(e), cc))
            def _():
                copy2(d, e).start()

        @pl.when(needs(r, cc))
        def _():
            copy3(d, 0).start()

    for d in range(1, C):
        cc = ctx_peer(d)
        pltpu.make_async_copy(pieces.at[cc, part(r)], pieces.at[cc, part(r)], pctx.at[cc]).wait()
    for e in range(1, half):
        piece2(e).start()
    piece3(0).start()

    @pl.loop(1, C)
    def _(d):
        @pl.when(needs(r, ctx_peer(d)))
        def _():
            @pl.loop(1, half)
            def _(e):
                arrived(ctx_peer(d), row_peer(e))
                copy3(d, e).start()

    for e in range(1, half):
        row_arrived(row_peer(e))
        piece3(e).start()

    @pl.loop(1, C)
    def _(d):
        cc = ctx_peer(d)

        @pl.when(needs(r, cc))
        def _():
            @pl.loop(0, half)
            def _(e):
                arrived(cc, other_row(e))

            @pl.loop(0, R // group)
            def _(g):
                process(kbuf, cc * shard + g * group * rows, cc * R + g * group)

    for e in range(half):
        row_arrived(other_row(e))

    def gathered(j):
        return jnp.concatenate(
            [pieces[i, pl.ds(j, R, stride=PIECE), :] for i in range(C)], axis=0
        )

    lanes_k = []
    for i in range(3):
        halves = [gathered(used + i * nb + j) for j in range(nb)]
        lanes_k.append(jnp.stack(halves, axis=1).reshape(TB, D))
    pooled = jnp.concatenate(lanes_k, axis=1)
    key_gate = fdot(pooled, gk_ref[...].astype(jnp.float32), ((1,), (0,)))
    row16 = lax.broadcasted_iota(jnp.int32, (PIECE, 1), 0)
    own = pieces[c, part(r), :]
    qg = jnp.zeros((PIECE, D), jnp.float32)
    qps, qgs = [], []
    for h in range(H):
        gate = gq_ref[h].astype(jnp.float32)
        qg = jnp.where(row16 // nb == h, fdot(own, gate, ((1,), (0,))), qg)
    logits = fdot(qg, key_gate, ((1,), (1,)))

    maps = jnp.full((PIECE, TB), NEG, jnp.float32)
    for h in range(H):
        pk = peak[h]
        top = jnp.max(pk, axis=0, keepdims=True)
        total = jnp.sum(bsum[h] * jnp.exp(pk - top), axis=0, keepdims=True)
        chance = (pk - (top + jnp.log(total))).T
        for j in range(nb):
            best = jnp.max(chance[j * BLK:(j + 1) * BLK], axis=0, keepdims=True)
            maps = jnp.where(row16 == h * nb + j, best, maps)
    allowed = maps > 0.01 * NEG
    block_map = jnp.where(allowed, jnp.exp(maps), 0.0)
    live = row16 < used
    gate_exp = jnp.where(allowed, jnp.exp(logits), 0.0)
    gate_sum = jnp.where(live, jnp.sum(gate_exp, axis=1, keepdims=True), 1.0)
    map_sum = jnp.where(live, jnp.sum(block_map, axis=1, keepdims=True), 1.0)
    diff = gate_exp / gate_sum - block_map / map_sum
    for h in range(H):
        for j in range(nb):
            diff_own[h:h + 1, j * TB:(j + 1) * TB] = diff[h * nb + j:h * nb + j + 1, :]

    def send(d, e):
        to_row, to_ctx = r + e, c + d
        to_row = jnp.where(to_row >= R, to_row - R, to_row)
        to_ctx = jnp.where(to_ctx >= C, to_ctx - C, to_ctx)
        return pltpu.make_async_remote_copy(
            src_ref=diff_own, dst_ref=diff_all.at[c * R + r],
            send_sem=ds1.at[0], recv_sem=dctx.at[0],
            device_id=(to_row, to_ctx), device_id_type=MESH,
        )

    for e in range(R - 1, -1, -1):
        for d in range(C - 1, -1, -1):
            if d or e:
                send(d, e).start()
    diff_all[c * R + r] = diff_own[...]
    for h in range(H):
        for j in range(nb):
            bm_ref[h, j:j + 1, :] = block_map[h * nb + j:h * nb + j + 1, :]


    for h in range(H):
        qp = jnp.concatenate([gathered(h * nb + j) for j in range(nb)], axis=0)
        qps.append(qp)
        qgs.append(fdot(qp, gq_ref[h].astype(jnp.float32), ((1,), (0,))))

    both = jnp.concatenate([key_gate] * nb, axis=0)
    wide_lane = lax.broadcasted_iota(jnp.int32, (1, nb * TB), 1)
    rest = diff_all.at[pl.ds(0, n - 1)]
    pltpu.make_async_copy(rest, rest, dctx.at[0]).wait()
    key_back = jnp.zeros((nb * TB, D), jnp.float32)
    for h in range(H):
        mixed = diff_all[:, h, :]
        diff = jnp.concatenate(
            [jnp.where(wide_lane // TB == j, mixed, 0.0) for j in range(nb)], axis=0
        )
        back = fdot(diff, both, ((1,), (0,)))
        dq_ref[h] = fdot(qps[h], back, ((0,), (0,)))
        key_back = key_back + fdot(diff, qgs[h], ((0,), (0,)))
    folded = key_back[:TB]
    for j in range(1, nb):
        folded = folded + key_back[j * TB:(j + 1) * TB]
    dk_ref[...] = fdot(pooled, folded, ((0,), (0,)))

    pltpu.make_async_copy(rest, rest, ds1.at[0]).wait()
    for d in range(1, C):
        cc = ctx_peer(d)
        copy1(d).wait_send()
        piece1(d).wait_send()
        for e in range(half):
            @pl.when(needs(r, cc))
            def _():
                copy3(d, e).wait_send()

            if e > 0:
                @pl.when(needs(row_peer(e), cc))
                def _():
                    copy2(d, e).wait_send()
    for e in range(half):
        piece3(e).wait_send()
        if e > 0:
            piece2(e).wait_send()


def shards(R, C, queries, keys, doc_ids, gate_query, gate_key):
    H, rows, D = queries.shape
    n = R * C
    nb = rows // BLK
    TB = doc_ids.shape[0]
    half = R // 2
    vm = pl.BlockSpec(memory_space=pltpu.VMEM)
    sm = pl.BlockSpec(memory_space=pltpu.SMEM)
    dma = pltpu.SemaphoreType.DMA
    return pl.pallas_call(
        functools.partial(kernel, R, C),
        out_shape=(
            jax.ShapeDtypeStruct((H, nb, TB), jnp.float32),
            jax.ShapeDtypeStruct((H, D, gate_query.shape[2]), jnp.float32),
            jax.ShapeDtypeStruct(gate_key.shape, jnp.float32),
        ),
        in_specs=[vm, vm, sm, vm, vm],
        out_specs=(vm, vm, vm),
        scratch_shapes=[
            pltpu.VMEM((C * keys.shape[0], D), jnp.bfloat16),
            pltpu.VMEM((D, H * rows), jnp.bfloat16),
            pltpu.VMEM((H, TB, rows), jnp.float32),
            pltpu.VMEM((H, TB, rows), jnp.float32),
            pltpu.VMEM((C, R * PIECE, D), jnp.float32),
            pltpu.VMEM((H, nb * TB), jnp.float32),
            pltpu.VMEM((n, H, nb * TB), jnp.float32),
            dma((C,)), dma((C * half,)), dma((C * half,)), dma((n,)),
            dma((C,)), dma((half,)), dma((half,)), dma((C,)), dma((R,)),
            dma((C,)), dma((R,)), dma((C,)), dma((R,)),
        ],
        compiler_params=pltpu.CompilerParams(
            collective_id=0, has_side_effects=True, vmem_limit_bytes=60 * 1024 * 1024
        ),
    )(queries, keys, doc_ids, gate_query, gate_key)


def solution(mesh):
    R, C = mesh.shape["row"], mesh.shape["ctx"]
    in_specs = (P(None, ("row", "ctx"), None), P("ctx", None), P(), P(), P())
    out_specs = (P(None, ("row", "ctx"), None), P(), P())
    return jax.shard_map(
        functools.partial(shards, R, C), mesh=mesh, in_specs=in_specs, out_specs=out_specs,
        check_vma=False,
    )
```

```python
import functools
import math

import jax
import jax.numpy as jnp
from jax import lax
from jax.experimental import pallas as pl
from jax.experimental.pallas import tpu as pltpu
from jax.sharding import PartitionSpec as P

BLK = 64
NEG = -1e30
PIECE = 16
GROUP = 4
MESH = pl.DeviceIdType.MESH
HI = lax.Precision.HIGHEST


def fdot(a, b, dims):
    return lax.dot_general(a, b, (dims, ((), ())), precision=HI, preferred_element_type=jnp.float32)


def kernel(
    R, C, q_ref, k_ref, doc_ref, gq_ref, gk_ref,
    bm_ref, qp_ref, qg_ref, both_ref, pooled_ref, diff_ref,
    kbuf, q_t, peak, bsum, pieces, diff_own, diff_all,
    s1, s2, s3, rsem, ps1, ps2, ps3, pctx, prow, ds1, ds2, dctx, drow,
):
    H, rows, D = q_ref.shape
    shard = k_ref.shape[0]
    nb = rows // BLK
    n = R * C
    TB = n * nb
    r = lax.axis_index("row")
    c = lax.axis_index("ctx")
    me = r * C + c
    half = R // 2
    scale = 1.0 / math.sqrt(D)
    used = H * nb

    def ctx_peer(d):
        return lax.rem(c + d, C)

    def row_peer(d):
        return lax.rem(r + 2 * d, R)

    partner = r + 1 - 2 * lax.rem(r, 2)

    def other_row(e):
        return lax.rem(partner + 2 * e, R)

    def needs(rr, cc):
        return cc * R < (rr // 2 + 1) * 2 * C

    barrier = pltpu.get_barrier_semaphore()
    for d in range(1, C):
        pl.semaphore_signal(barrier, inc=1, device_id=(r, ctx_peer(d)), device_id_type=MESH)
    for d in range(1, half):
        pl.semaphore_signal(barrier, inc=1, device_id=(row_peer(d), c), device_id_type=MESH)
    pl.semaphore_signal(barrier, inc=1, device_id=(partner, c), device_id_type=MESH)

    def slot(cc, rr):
        return pl.ds(pl.multiple_of(cc * shard + rr * rows, rows), rows)

    def part(rr):
        return pl.ds(pl.multiple_of(rr * PIECE, PIECE), PIECE)

    for h in range(H):
        qf = q_ref[h].astype(jnp.float32)
        q_t[:, h * rows:(h + 1) * rows] = qf.T.astype(jnp.bfloat16)
        for j in range(nb):
            pieces[c, pl.ds(r * PIECE + h * nb + j, 1), :] = jnp.mean(
                qf[j * BLK:(j + 1) * BLK], axis=0, keepdims=True
            )
    wide = k_ref[pl.ds(pl.multiple_of(r * rows, rows), rows), :].astype(jnp.float32)
    for j in range(nb):
        t = wide[j * BLK:(j + 1) * BLK]
        for i, pool in enumerate((jnp.max, jnp.min, jnp.mean)):
            pieces[c, pl.ds(r * PIECE + used + i * nb + j, 1), :] = pool(
                t, axis=0, keepdims=True
            )
    peak[...] = jnp.full_like(peak, NEG)
    bsum[...] = jnp.zeros_like(bsum)

    a0 = me * nb
    lane = lax.broadcasted_iota(jnp.int32, (1, rows), 1)
    qdoc = jnp.zeros((1, rows), jnp.int32)
    for j in range(nb):
        qdoc = jnp.where(lane // BLK == j, doc_ref[a0 + j], qdoc)

    def score(num, keys, diagonal):
        for h in range(H):
            s = jnp.dot(
                keys, q_t[:, h * rows:(h + 1) * rows], preferred_element_type=jnp.float32
            )
            if diagonal:
                ki = lax.broadcasted_iota(jnp.int32, (rows, rows), 0)
                qi = lax.broadcasted_iota(jnp.int32, (rows, rows), 1)
                s = jnp.where(ki <= qi, s, NEG)
            for j in range(keys.shape[0] // BLK):
                b = num * nb + j
                t = s[j * BLK:(j + 1) * BLK]
                top = jnp.max(t, axis=0, keepdims=True)
                total = jnp.sum(
                    jnp.exp2((t - top) * (scale * math.log2(math.e))), axis=0, keepdims=True
                )
                peak[h, pl.ds(b, 1), :] = jnp.where(qdoc == doc_ref[b], top * scale, NEG)
                bsum[h, pl.ds(b, 1), :] = total

    group = math.gcd(R, GROUP)

    def process(ref, base, first):
        @pl.when(first + group <= me)
        def _():
            for i in range(0, group, 2):
                at = pl.multiple_of(base + i * rows, rows)
                score(first + i, ref[pl.ds(at, 2 * rows), :], False)

        @pl.when(first + group > me)
        def _():
            @pl.loop(0, group)
            def _(i):
                at = pl.ds(pl.multiple_of(base + i * rows, rows), rows)

                @pl.when(first + i < me)
                def _():
                    score(first + i, ref[at, :], False)

                @pl.when(first + i == me)
                def _():
                    score(first + i, ref[at, :], True)

    @pl.loop(0, R // group)
    def _(g):
        process(k_ref, g * group * rows, c * R + g * group)

    pl.semaphore_wait(barrier, C - 1 + half)

    def copy1(d):
        return pltpu.make_async_remote_copy(
            src_ref=k_ref.at[pl.ds(pl.multiple_of(r * rows, rows), rows)],
            dst_ref=kbuf.at[slot(c, r)],
            send_sem=s1.at[d], recv_sem=rsem.at[c * R + r],
            device_id=(r, ctx_peer(d)), device_id_type=MESH,
        )

    def copy2(d, e):
        cc = ctx_peer(d)
        return pltpu.make_async_remote_copy(
            src_ref=kbuf.at[slot(cc, r)], dst_ref=kbuf.at[slot(cc, r)],
            send_sem=s2.at[d * half + e], recv_sem=rsem.at[cc * R + r],
            device_id=(row_peer(e), c), device_id_type=MESH,
        )

    def copy3(d, e):
        cc, rr = ctx_peer(d), row_peer(e)
        return pltpu.make_async_remote_copy(
            src_ref=kbuf.at[slot(cc, rr)], dst_ref=kbuf.at[slot(cc, rr)],
            send_sem=s3.at[d * half + e], recv_sem=rsem.at[cc * R + rr],
            device_id=(partner, c), device_id_type=MESH,
        )

    def arrived(cc, rr):
        pltpu.make_async_copy(
            kbuf.at[slot(cc, rr)], kbuf.at[slot(cc, rr)], rsem.at[cc * R + rr]
        ).wait()

    def piece1(d):
        return pltpu.make_async_remote_copy(
            src_ref=pieces.at[c, part(r)], dst_ref=pieces.at[c, part(r)],
            send_sem=ps1.at[d], recv_sem=pctx.at[c],
            device_id=(r, ctx_peer(d)), device_id_type=MESH,
        )

    def piece2(e):
        return pltpu.make_async_remote_copy(
            src_ref=pieces.at[:, part(r)], dst_ref=pieces.at[:, part(r)],
            send_sem=ps2.at[e], recv_sem=prow.at[r],
            device_id=(row_peer(e), c), device_id_type=MESH,
        )

    def piece3(e):
        rr = row_peer(e)
        return pltpu.make_async_remote_copy(
            src_ref=pieces.at[:, part(rr)], dst_ref=pieces.at[:, part(rr)],
            send_sem=ps3.at[e], recv_sem=prow.at[rr],
            device_id=(partner, c), device_id_type=MESH,
        )

    def row_arrived(rr):
        pltpu.make_async_copy(
            pieces.at[:, part(rr)], pieces.at[:, part(rr)], prow.at[rr]
        ).wait()

    for d in range(1, C):
        piece1(d).start()
    for d in range(1, C):
        copy1(d).start()

    for d in range(1, C):
        cc = ctx_peer(d)
        pltpu.make_async_copy(pieces.at[cc, part(r)], pieces.at[cc, part(r)], pctx.at[cc]).wait()
    for e in range(1, half):
        piece2(e).start()
    piece3(0).start()

    for d in range(1, C):
        cc = ctx_peer(d)
        arrived(cc, r)
        for e in range(1, half):
            @pl.when(needs(row_peer(e), cc))
            def _():
                copy2(d, e).start()

        @pl.when(needs(r, cc))
        def _():
            copy3(d, 0).start()

    for e in range(1, half):
        row_arrived(row_peer(e))
        piece3(e).start()

    @pl.loop(1, C)
    def _(d):
        @pl.when(needs(r, ctx_peer(d)))
        def _():
            @pl.loop(1, half)
            def _(e):
                arrived(ctx_peer(d), row_peer(e))
                copy3(d, e).start()

    for e in range(half):
        row_arrived(other_row(e))

    def gathered(j):
        return jnp.concatenate(
            [pieces[i, pl.ds(j, R, stride=PIECE), :] for i in range(C)], axis=0
        )

    lanes_k = []
    for i in range(3):
        halves = [gathered(used + i * nb + j) for j in range(nb)]
        lanes_k.append(jnp.stack(halves, axis=1).reshape(TB, D))
    pooled = jnp.concatenate(lanes_k, axis=1)
    key_gate = fdot(pooled, gk_ref[...].astype(jnp.float32), ((1,), (0,)))
    row16 = lax.broadcasted_iota(jnp.int32, (PIECE, 1), 0)
    own = pieces[c, part(r), :]
    qg = jnp.zeros((PIECE, D), jnp.float32)
    for h in range(H):
        gate = gq_ref[h].astype(jnp.float32)
        qg = jnp.where(row16 // nb == h, fdot(own, gate, ((1,), (0,))), qg)
    logits = fdot(qg, key_gate, ((1,), (1,)))

    @pl.loop(1, C)
    def _(d):
        cc = ctx_peer(d)

        @pl.when(needs(r, cc))
        def _():
            @pl.loop(0, half)
            def _(e):
                arrived(cc, other_row(e))

            @pl.loop(0, R // group)
            def _(g):
                process(kbuf, cc * shard + g * group * rows, cc * R + g * group)

    maps = jnp.full((PIECE, TB), NEG, jnp.float32)
    for h in range(H):
        pk = peak[h]
        top = jnp.max(pk, axis=0, keepdims=True)
        total = jnp.sum(bsum[h] * jnp.exp(pk - top), axis=0, keepdims=True)
        chance = (pk - (top + jnp.log(total))).T
        for j in range(nb):
            best = jnp.max(chance[j * BLK:(j + 1) * BLK], axis=0, keepdims=True)
            maps = jnp.where(row16 == h * nb + j, best, maps)
    allowed = maps > 0.01 * NEG
    block_map = jnp.where(allowed, jnp.exp(maps), 0.0)
    live = row16 < used
    gate_exp = jnp.where(allowed, jnp.exp(logits), 0.0)
    gate_sum = jnp.where(live, jnp.sum(gate_exp, axis=1, keepdims=True), 1.0)
    map_sum = jnp.where(live, jnp.sum(block_map, axis=1, keepdims=True), 1.0)
    diff = gate_exp / gate_sum - block_map / map_sum
    for h in range(H):
        for j in range(nb):
            diff_own[h:h + 1, j * TB:(j + 1) * TB] = diff[h * nb + j:h * nb + j + 1, :]

    def send(d, e):
        to_row, to_ctx = r + e, c + d
        to_row = jnp.where(to_row >= R, to_row - R, to_row)
        to_ctx = jnp.where(to_ctx >= C, to_ctx - C, to_ctx)
        return pltpu.make_async_remote_copy(
            src_ref=diff_own, dst_ref=diff_all.at[c * R + r],
            send_sem=ds1.at[0], recv_sem=dctx.at[0],
            device_id=(to_row, to_ctx), device_id_type=MESH,
        )

    for e in range(R - 1, -1, -1):
        for d in range(C - 1, -1, -1):
            if d or e:
                send(d, e).start()
    diff_all[c * R + r] = diff_own[...]
    for h in range(H):
        for j in range(nb):
            bm_ref[h, j:j + 1, :] = block_map[h * nb + j:h * nb + j + 1, :]


    for h in range(H):
        qp = jnp.concatenate([gathered(h * nb + j) for j in range(nb)], axis=0)
        qp_ref[h] = qp
        qg_ref[h] = fdot(qp, gq_ref[h].astype(jnp.float32), ((1,), (0,)))

    for j in range(nb):
        both_ref[j * TB:(j + 1) * TB] = key_gate
    pooled_ref[...] = pooled
    rest = diff_all.at[pl.ds(0, n - 1)]
    pltpu.make_async_copy(rest, rest, dctx.at[0]).wait()
    diff_ref[...] = diff_all[...]
    pltpu.make_async_copy(rest, rest, ds1.at[0]).wait()
    for d in range(1, C):
        cc = ctx_peer(d)
        copy1(d).wait_send()
        piece1(d).wait_send()
        for e in range(half):
            @pl.when(needs(r, cc))
            def _():
                copy3(d, e).wait_send()

            if e > 0:
                @pl.when(needs(row_peer(e), cc))
                def _():
                    copy2(d, e).wait_send()
    for e in range(half):
        piece3(e).wait_send()
        if e > 0:
            piece2(e).wait_send()


def finish(map_ref, qp_ref, qg_ref, both_ref, pooled_ref, diff_ref, bm_ref, dq_ref, dk_ref):
    H, nb, TB = map_ref.shape
    bm_ref[...] = map_ref[...]
    both = both_ref[...]
    wide_lane = lax.broadcasted_iota(jnp.int32, (1, nb * TB), 1)
    key_back = jnp.zeros(both.shape, jnp.float32)
    for h in range(H):
        mixed = diff_ref[:, h, :]
        diff = jnp.concatenate(
            [jnp.where(wide_lane // TB == j, mixed, 0.0) for j in range(nb)], axis=0
        )
        back = fdot(diff, both, ((1,), (0,)))
        dq_ref[h] = fdot(qp_ref[h], back, ((0,), (0,)))
        key_back = key_back + fdot(diff, qg_ref[h], ((0,), (0,)))
    folded = key_back[:TB]
    for j in range(1, nb):
        folded = folded + key_back[j * TB:(j + 1) * TB]
    dk_ref[...] = fdot(pooled_ref[...], folded, ((0,), (0,)))


def shards(R, C, queries, keys, doc_ids, gate_query, gate_key):
    H, rows, D = queries.shape
    n = R * C
    nb = rows // BLK
    TB = doc_ids.shape[0]
    half = R // 2
    vm = pl.BlockSpec(memory_space=pltpu.VMEM)
    sm = pl.BlockSpec(memory_space=pltpu.SMEM)
    dma = pltpu.SemaphoreType.DMA
    parts = pl.pallas_call(
        functools.partial(kernel, R, C),
        out_shape=(
            jax.ShapeDtypeStruct((H, nb, TB), jnp.float32),
            jax.ShapeDtypeStruct((H, nb * n, D), jnp.float32),
            jax.ShapeDtypeStruct((H, nb * n, D), jnp.float32),
            jax.ShapeDtypeStruct((nb * TB, D), jnp.float32),
            jax.ShapeDtypeStruct((TB, 3 * D), jnp.float32),
            jax.ShapeDtypeStruct((n, H, nb * TB), jnp.float32),
        ),
        in_specs=[vm, vm, sm, vm, vm],
        out_specs=(vm,) * 6,
        scratch_shapes=[
            pltpu.VMEM((C * keys.shape[0], D), jnp.bfloat16),
            pltpu.VMEM((D, H * rows), jnp.bfloat16),
            pltpu.VMEM((H, TB, rows), jnp.float32),
            pltpu.VMEM((H, TB, rows), jnp.float32),
            pltpu.VMEM((C, R * PIECE, D), jnp.float32),
            pltpu.VMEM((H, nb * TB), jnp.float32),
            pltpu.VMEM((n, H, nb * TB), jnp.float32),
            dma((C,)), dma((C * half,)), dma((C * half,)), dma((n,)),
            dma((C,)), dma((half,)), dma((half,)), dma((C,)), dma((R,)),
            dma((C,)), dma((R,)), dma((C,)), dma((R,)),
        ],
        compiler_params=pltpu.CompilerParams(
            collective_id=0, has_side_effects=True, vmem_limit_bytes=60 * 1024 * 1024
        ),
    )(queries, keys, doc_ids, gate_query, gate_key)
    return pl.pallas_call(
        finish,
        out_shape=(
            jax.ShapeDtypeStruct((H, nb, TB), jnp.float32),
            jax.ShapeDtypeStruct(gate_query.shape, jnp.float32),
            jax.ShapeDtypeStruct(gate_key.shape, jnp.float32),
        ),
        in_specs=[vm] * 6,
        out_specs=(vm,) * 3,
        compiler_params=pltpu.CompilerParams(vmem_limit_bytes=60 * 1024 * 1024),
    )(*parts)


def solution(mesh):
    R, C = mesh.shape["row"], mesh.shape["ctx"]
    in_specs = (P(None, ("row", "ctx"), None), P("ctx", None), P(), P(), P())
    out_specs = (P(None, ("row", "ctx"), None), P(), P())
    return jax.shard_map(
        functools.partial(shards, R, C), mesh=mesh, in_specs=in_specs, out_specs=out_specs,
        check_vma=False,
    )
```
